256 devices in a mesh: node: 32 (over z, y), head: 8 (over x, core).
Axes of the slice: x: 4, y: 4, z: 8, core: 2. Of those that a mesh axis runs over, the one named last changes fastest.
Arguments:
- query_rows: bfloat16 [32768, 1024], P(('node', 'head')), may hold values from -6 to 6
- key_rows: bfloat16 [32768, 1024], P(('node', 'head')), may hold values from -6 to 6
- value_rows: bfloat16 [32768, 1024], P(('node', 'head')), may hold values from -6 to 6
- grad_out: bfloat16 [32768, 1024], P(('node', 'head')), may hold values from -6 to 6
- heat_bias: bfloat16 [256, 16, 128, 128], P('node'), may hold values from -5 to 5
- block_pattern: int32 [256, 16], P('node'), may hold values from -1 to 255, as said below
Outputs:
- grad_query: bfloat16 [32768, 1024], P(('node', 'head'))
- grad_key: bfloat16 [32768, 1024], P(('node', 'head'))
- grad_value: bfloat16 [32768, 1024], P(('node', 'head'))
The draws below stay inside these ranges and needn't reach their ends.
Inputs may be any that keep to these rules, and one draw needn't show every extreme that they name: `block_pattern`: entry (c, j) names a key cluster of query cluster c or is -1 for an empty slot; slot 0 names c itself, and every named cluster c2 has c2 // 8 within 2 of c // 8.
All inputs are finite; a program needn't handle non-finite values.
Results may differ from the reference program's by a relative error of at most 0.011.
Values may be sent and summed in bfloat16 or wider, within the bound.
A program may use at most 128 MiB of HBM per device.

```python
import jax
import jax.numpy as jnp
from jax import lax

CL = 128
H = 16
HDIM = 64
NB = 16
REACH = 2
CPN = 8
CLUSTERS = 256
NODES = 32768
FEAT = 1024


def shared_rows(key, which):
    shape = (NODES, H * HDIM)
    base = jax.random.normal(jax.random.fold_in(key, 101 + which), shape, jnp.float32)
    return jnp.clip(1.5 * base, -6.0, 6.0)


def draw_query_rows(key, part):
    return shared_rows(key, 0).astype(jnp.bfloat16)


def draw_key_rows(key, part):
    return shared_rows(key, 1).astype(jnp.bfloat16)


def draw_block_pattern(key, part):
    shape = (CLUSTERS, NB)
    shards = CLUSTERS // CPN
    cluster = lax.broadcasted_iota(jnp.int32, shape, 0)
    slot = lax.broadcasted_iota(jnp.int32, shape, 1)
    home = cluster // CPN
    fixed_offset = jnp.where(slot <= REACH, slot - REACH - 1, slot - REACH)
    extra_offset = jax.random.randint(jax.random.fold_in(key, 31), shape, -REACH, REACH + 1)
    offset = jnp.where(slot <= 2 * REACH, fixed_offset, extra_offset)
    target = home + offset
    inside = (target >= 0) & (target < shards)
    clipped = jnp.clip(target, 0, shards - 1)
    pick = jax.random.randint(jax.random.fold_in(key, 32), shape, 0, CPN)
    named = clipped * CPN + pick
    keep = jax.random.randint(jax.random.fold_in(key, 33), shape, 0, 4) > 0
    result = jnp.where(slot <= 2 * REACH, jnp.where(inside, named, -1), jnp.where(keep, named, -1))
    return jnp.where(slot == 0, cluster, result).astype(jnp.int32)


def levels(key, extent, cuts, least, top_value):
    gain, own = 1.0, jax.random.fold_in(key, 6)
    for axis_at, blocks in cuts:
        steps = jnp.exp(jax.random.uniform(jax.random.fold_in(own, axis_at), (blocks,), jnp.float32, least / len(cuts), top_value / len(cuts)))
        gain = gain * jnp.repeat(steps, extent[axis_at] // blocks).reshape([-1 if axis == axis_at else 1 for axis in range(len(extent))])
    return gain


def scatter_about(stream_key, shape, width, bound, split=(), held_as=jnp.bfloat16):
    array = width * jax.random.normal(stream_key, shape, jnp.float32)
    if split:
        array = array * levels(stream_key, shape, split, -0.22, 0.18)
    return jnp.clip(array, -bound, bound).astype(held_as)


def setup_inputs(seed: int = 0) -> dict:
    splits = jax.random.split(jax.random.key(seed), 7)
    query_rows = draw_query_rows(jax.random.fold_in(splits[6], 71), 0)
    key_rows = draw_key_rows(jax.random.fold_in(splits[6], 71), 0)
    value_rows = scatter_about(splits[2], (NODES, FEAT), 1.0, 6.0, ((0, 256),))
    grad_out = scatter_about(splits[3], (NODES, FEAT), 1.0, 6.0, ((0, 256),))
    heat_bias = scatter_about(splits[4], (CLUSTERS, NB, CL, CL), 1.0, 5.0, ((0, 32),))
    block_pattern = draw_block_pattern(jax.random.fold_in(splits[6], 71), 0)
    return {"query_rows": query_rows, "key_rows": key_rows, "value_rows": value_rows, "grad_out": grad_out, "heat_bias": heat_bias, "block_pattern": block_pattern}


def reference(query_rows, key_rows, value_rows, grad_out, heat_bias, block_pattern):
    scale = HDIM ** -0.5
    queries = query_rows.reshape(CLUSTERS, CL, H, HDIM)
    keys_all = key_rows.reshape(CLUSTERS, CL, H, HDIM).astype(jnp.float32)
    values_all = value_rows.reshape(CLUSTERS, CL, H, HDIM).astype(jnp.float32)
    cotangent = grad_out.reshape(CLUSTERS, CL, H, HDIM)

    def advance(carry, inputs):
        grad_k, grad_v = carry
        q_blk, g_blk, b_blk, pattern_row = inputs
        valid = pattern_row >= 0
        index = jnp.where(valid, pattern_row, 0).astype(jnp.int32)
        k_blk = keys_all[index]
        v_blk = values_all[index]
        q_f = q_blk.astype(jnp.float32)
        g_f = g_blk.astype(jnp.float32)
        scores = jnp.einsum('rhd,jchd->hrjc', q_f, k_blk) * scale
        scores = scores + jnp.transpose(b_blk.astype(jnp.float32), (1, 0, 2))[None]
        scores = jnp.where(valid[None, None, :, None], scores, -jnp.inf)
        top = jnp.max(scores, axis=(2, 3), keepdims=True)
        prob = jnp.exp(scores - top)
        prob = prob / jnp.sum(prob, axis=(2, 3), keepdims=True)
        prob_half = lax.optimization_barrier(prob.astype(jnp.bfloat16)).astype(jnp.float32)
        attended = jnp.einsum('hrjc,jchd->rhd', prob_half, v_blk)
        delta = jnp.sum(g_f * attended, axis=2)
        dprob = jnp.einsum('rhd,jchd->hrjc', g_f, v_blk)
        dscore = prob * (dprob - jnp.transpose(delta)[:, :, None, None])
        dscore_half = lax.optimization_barrier(dscore.astype(jnp.bfloat16)).astype(jnp.float32)
        grad_q = jnp.einsum('hrjc,jchd->rhd', dscore_half, k_blk) * scale
        part_k = jnp.einsum('hrjc,rhd->jchd', dscore_half, q_f) * scale
        part_v = jnp.einsum('hrjc,rhd->jchd', prob_half, g_f)
        grad_k = grad_k.at[index].add(part_k)
        grad_v = grad_v.at[index].add(part_v)
        return (grad_k, grad_v), grad_q

    start = (jnp.zeros((CLUSTERS, CL, H, HDIM), jnp.float32), jnp.zeros((CLUSTERS, CL, H, HDIM), jnp.float32))
    (grad_k, grad_v), grad_q = lax.scan(advance, start, (queries, cotangent, heat_bias, block_pattern))
    shape = (NODES, H * HDIM)
    return (grad_q.reshape(shape).astype(jnp.bfloat16), grad_k.reshape(shape).astype(jnp.bfloat16), grad_v.reshape(shape).astype(jnp.bfloat16))
```

```python
import functools

import jax
import jax.numpy as jnp
from jax import lax
from jax.experimental import pallas as pl
from jax.experimental.pallas import tpu as pltpu
from jax.sharding import PartitionSpec as P

CL=128; NB=16; CPN=8; NEAR=40; HDIM=64
NT = (((1,), (1,)), ((), ()))
TN = (((0,), (0,)), ((), ()))
NN = (((1,), (0,)), ((), ()))

def two_heads(x):
    lane = lax.broadcasted_iota(jnp.int32, x.shape, 1)
    zero = jnp.zeros_like(x)
    return jnp.concatenate([jnp.where(lane < HDIM, x, zero), jnp.where(lane < HDIM, zero, x)], axis=0)

def dot(a, b, dims):
    return lax.dot_general(a, b, dims, preferred_element_type=jnp.float32)

def fold(x, op):
    return op(x.reshape(x.shape[0] // 8, 8, x.shape[1]), axis=0)

def attend_kernel(idx_ref, q_ref, g_ref, b_ref, k_ref, v_ref, gq_ref, gk_ref, gv_ref, kg, vg, s, dp, acck, accv, *, CH):
    i = pl.program_id(0)
    @pl.when(i == 0)
    def _():
        acck[...] = jnp.zeros_like(acck)
        accv[...] = jnp.zeros_like(accv)
    q2 = two_heads(q_ref[0] * jnp.bfloat16(0.125))
    g2 = two_heads(g_ref[0])
    R = CH * CL
    def slot(j):
        raw = idx_ref[i * NB + j]
        return jnp.where(raw < 0, 16 + i, raw), jnp.where(raw < 0, jnp.float32(-1e30), jnp.float32(0))
    def first(c, top):
        pens = []
        for u in range(CH):
            at, pen = slot(c * CH + u)
            pens.append(pen)
            kg[pl.ds(pl.multiple_of(c * R + u * CL, CL), CL), :] = k_ref[at]
            vg[pl.ds(pl.multiple_of(c * R + u * CL, CL), CL), :] = v_ref[at]
        rows = pl.ds(pl.multiple_of(c * R, R), R)
        st = dot(kg[rows, :], q2, NT)
        for u in range(CH):
            bt = b_ref[0, c * CH + u].astype(jnp.float32).T + pens[u]
            x = st[u * CL:(u + 1) * CL] + jnp.concatenate([bt, bt], axis=1)
            s[pl.ds(pl.multiple_of(c * R + u * CL, CL), CL), :] = x
            top = jnp.maximum(top, fold(x, jnp.max))
        return top
    top = lax.fori_loop(0, NB // CH, first, jnp.full((8, 2 * CL), -jnp.inf, jnp.float32))
    top = jnp.max(top, axis=0, keepdims=True)
    def second(c, carry):
        total, delta = carry
        rows = pl.ds(pl.multiple_of(c * R, R), R)
        d = dot(vg[rows, :], g2, NT)
        e = jnp.exp(s[rows, :] - top)
        s[rows, :] = e
        dp[rows, :] = d
        return total + fold(e, jnp.sum), delta + fold(e * d, jnp.sum)
    zero = jnp.zeros((8, 2 * CL), jnp.float32)
    total, delta = lax.fori_loop(0, NB // CH, second, (zero, zero))
    inv = 1.0 / jnp.sum(total, axis=0, keepdims=True)
    delta = jnp.sum(delta, axis=0, keepdims=True) * inv
    def third(c, gqt):
        rows = pl.ds(pl.multiple_of(c * R, R), R)
        p = s[rows, :] * inv
        ph = p.astype(jnp.bfloat16)
        ds = (p * (dp[rows, :] - delta)).astype(jnp.bfloat16)
        pv = dot(ph, g2, NN)
        pk = dot(ds, q2, NN)
        for u in range(CH):
            at, _ = slot(c * CH + u)
            accv[at] += pv[u * CL:(u + 1) * CL]
            acck[at] += pk[u * CL:(u + 1) * CL]
        return gqt + dot(kg[rows, :], ds, TN)
    gqt = lax.fori_loop(0, NB // CH, third, jnp.zeros((CL, 2 * CL), jnp.float32))
    gqt = jnp.concatenate([gqt[:HDIM, :CL], gqt[HDIM:, CL:]], axis=0) * 0.125
    gq_ref[0] = gqt.T.astype(jnp.bfloat16)
    @pl.when(i == CPN - 1)
    def _():
        gk_ref[...] = acck[...].astype(jnp.bfloat16)
        gv_ref[...] = accv[...].astype(jnp.bfloat16)

def attend(index, q, g, bias, near_k, near_v, CH=8):
    bf = jnp.bfloat16
    whole = pl.BlockSpec((NEAR, CL, CL), lambda i, x: (0, 0, 0), pipeline_mode=pl.Buffered(1))
    one = pl.BlockSpec((1, CL, CL), lambda i, x: (i, 0, 0))
    return pl.pallas_call(
        functools.partial(attend_kernel, CH=CH),
        out_shape=(jax.ShapeDtypeStruct((CPN, CL, CL), bf), jax.ShapeDtypeStruct((NEAR, CL, CL), bf), jax.ShapeDtypeStruct((NEAR, CL, CL), bf)),
        grid_spec=pltpu.PrefetchScalarGridSpec(
            num_scalar_prefetch=1, grid=(CPN,),
            in_specs=[one, one, pl.BlockSpec((1, NB, CL, CL), lambda i, x: (i, 0, 0, 0)), whole, whole],
            out_specs=[one, whole, whole],
            scratch_shapes=[pltpu.VMEM((NB * CL, CL), bf), pltpu.VMEM((NB * CL, CL), bf), pltpu.VMEM((NB * CL, 2 * CL), jnp.float32), pltpu.VMEM((NB * CL, 2 * CL), jnp.float32), pltpu.VMEM((NEAR, CL, CL), jnp.float32), pltpu.VMEM((NEAR, CL, CL), jnp.float32)]),
        compiler_params=pltpu.CompilerParams(dimension_semantics=("arbitrary",)),
    )(index, q, g, bias, near_k, near_v)


REACH = 2


def shifted(array, axis, by):
    size = lax.axis_size(axis)
    pairs = [(i, i + by) for i in range(size) if 0 <= i + by < size]
    return lax.ppermute(array, axis, pairs)


def on_device(query_rows, key_rows, value_rows, grad_out, heat_bias, block_pattern):
    def enter(a):
        return lax.all_to_all(a, "head", split_axis=1, concat_axis=0, tiled=True).reshape(CPN, CL, CL)

    def leave(a):
        return lax.all_to_all(a.reshape(CPN * CL, CL), "head", split_axis=0, concat_axis=1, tiled=True)

    k, v, q, g = enter(key_rows), enter(value_rows), enter(query_rows), enter(grad_out)
    shard = lax.axis_index("node")
    offsets = list(range(-REACH, REACH + 1))
    near_k = jnp.concatenate([k if o == 0 else shifted(k, "node", -o) for o in offsets], axis=0)
    near_v = jnp.concatenate([v if o == 0 else shifted(v, "node", -o) for o in offsets], axis=0)
    index = jnp.where(block_pattern < 0, -1, block_pattern - (shard - REACH) * CPN).reshape(-1)
    gq, gk, gv = attend(index, q, g, heat_bias, near_k, near_v)

    def total(parts):
        acc = parts[REACH * CPN : (REACH + 1) * CPN].astype(jnp.float32)
        for o in offsets:
            if o != 0:
                first = (o + REACH) * CPN
                acc = acc + shifted(parts[first : first + CPN], "node", o).astype(jnp.float32)
        return acc.astype(jnp.bfloat16)

    return leave(gq), leave(total(gk)), leave(total(gv))


def solution(mesh):
    rows = P(("node", "head"), None)
    return jax.shard_map(
        on_device,
        mesh=mesh,
        in_specs=(rows, rows, rows, rows, P("node", None, None, None), P("node", None)),
        out_specs=(rows, rows, rows),
        check_vma=False,
    )
```

```python
import functools

import jax
import jax.numpy as jnp
from jax import lax
from jax.experimental import pallas as pl
from jax.experimental.pallas import tpu as pltpu
from jax.sharding import PartitionSpec as P

CL=128; NB=16; CPN=8; NEAR=40; HDIM=64
NT = (((1,), (1,)), ((), ()))
TN = (((0,), (0,)), ((), ()))
NN = (((1,), (0,)), ((), ()))

def two_heads(x):
    lane = lax.broadcasted_iota(jnp.int32, x.shape, 1)
    zero = jnp.zeros_like(x)
    return jnp.concatenate([jnp.where(lane < HDIM, x, zero), jnp.where(lane < HDIM, zero, x)], axis=0)

def dot(a, b, dims):
    return lax.dot_general(a, b, dims, preferred_element_type=jnp.float32)

def fold(x, op):
    return op(x.reshape(x.shape[0] // 8, 8, x.shape[1]), axis=0)

def attend_kernel(idx_ref, q_ref, g_ref, b_ref, k_ref, v_ref, gq_ref, gk_ref, gv_ref, kg, vg, s, dp, acck, accv, *, CH):
    i = pl.program_id(0)
    @pl.when(i == 0)
    def _():
        acck[...] = jnp.zeros_like(acck)
        accv[...] = jnp.zeros_like(accv)
    q2 = two_heads(q_ref[0] * jnp.bfloat16(0.125))
    g2 = two_heads(g_ref[0])
    R = CH * CL
    def slot(j):
        raw = idx_ref[i * NB + j]
        return jnp.where(raw < 0, 16 + i, raw), jnp.where(raw < 0, jnp.float32(-1e30), jnp.float32(0))
    def first(c, top):
        pens = []
        for u in range(CH):
            at, pen = slot(c * CH + u)
            pens.append(pen)
            kg[pl.ds(pl.multiple_of(c * R + u * CL, CL), CL), :] = k_ref[at]
            vg[pl.ds(pl.multiple_of(c * R + u * CL, CL), CL), :] = v_ref[at]
        rows = pl.ds(pl.multiple_of(c * R, R), R)
        st = dot(kg[rows, :], q2, NT)
        for u in range(CH):
            bt = b_ref[0, c * CH + u].astype(jnp.float32).T + pens[u]
            x = st[u * CL:(u + 1) * CL] + jnp.concatenate([bt, bt], axis=1)
            s[pl.ds(pl.multiple_of(c * R + u * CL, CL), CL), :] = x
            top = jnp.maximum(top, fold(x, jnp.max))
        return top
    top = lax.fori_loop(0, NB // CH, first, jnp.full((8, 2 * CL), -jnp.inf, jnp.float32))
    top = jnp.max(top, axis=0, keepdims=True)
    def second(c, carry):
        total, delta = carry
        rows = pl.ds(pl.multiple_of(c * R, R), R)
        d = dot(vg[rows, :], g2, NT)
        e = jnp.exp(s[rows, :] - top)
        s[rows, :] = e
        dp[rows, :] = d
        return total + fold(e, jnp.sum), delta + fold(e * d, jnp.sum)
    zero = jnp.zeros((8, 2 * CL), jnp.float32)
    total, delta = lax.fori_loop(0, NB // CH, second, (zero, zero))
    inv = 1.0 / jnp.sum(total, axis=0, keepdims=True)
    delta = jnp.sum(delta, axis=0, keepdims=True) * inv
    def third(c, gqt):
        rows = pl.ds(pl.multiple_of(c * R, R), R)
        p = s[rows, :] * inv
        ph = p.astype(jnp.bfloat16)
        ds = (p * (dp[rows, :] - delta)).astype(jnp.bfloat16)
        pv = dot(ph, g2, NN)
        pk = dot(ds, q2, NN)
        for u in range(CH):
            at, _ = slot(c * CH + u)
            accv[at] += pv[u * CL:(u + 1) * CL]
            acck[at] += pk[u * CL:(u + 1) * CL]
        return gqt + dot(kg[rows, :], ds, TN)
    gqt = lax.fori_loop(0, NB // CH, third, jnp.zeros((CL, 2 * CL), jnp.float32))
    gqt = jnp.concatenate([gqt[:HDIM, :CL], gqt[HDIM:, CL:]], axis=0) * 0.125
    gq_ref[0] = gqt.T.astype(jnp.bfloat16)
    @pl.when(i == CPN - 1)
    def _():
        gk_ref[...] = acck[...].astype(jnp.bfloat16)
        gv_ref[...] = accv[...].astype(jnp.bfloat16)

def attend(index, q, g, bias, near_k, near_v, CH=8):
    bf = jnp.bfloat16
    whole = pl.BlockSpec((NEAR, CL, CL), lambda i, x: (0, 0, 0), pipeline_mode=pl.Buffered(1))
    one = pl.BlockSpec((1, CL, CL), lambda i, x: (i, 0, 0))
    return pl.pallas_call(
        functools.partial(attend_kernel, CH=CH),
        out_shape=(jax.ShapeDtypeStruct((CPN, CL, CL), bf), jax.ShapeDtypeStruct((NEAR, CL, CL), bf), jax.ShapeDtypeStruct((NEAR, CL, CL), bf)),
        grid_spec=pltpu.PrefetchScalarGridSpec(
            num_scalar_prefetch=1, grid=(CPN,),
            in_specs=[one, one, pl.BlockSpec((1, NB, CL, CL), lambda i, x: (i, 0, 0, 0)), whole, whole],
            out_specs=[one, whole, whole],
            scratch_shapes=[pltpu.VMEM((NB * CL, CL), bf), pltpu.VMEM((NB * CL, CL), bf), pltpu.VMEM((NB * CL, 2 * CL), jnp.float32), pltpu.VMEM((NB * CL, 2 * CL), jnp.float32), pltpu.VMEM((NEAR, CL, CL), jnp.float32), pltpu.VMEM((NEAR, CL, CL), jnp.float32)]),
        compiler_params=pltpu.CompilerParams(dimension_semantics=("arbitrary",)),
    )(index, q, g, bias, near_k, near_v)


REACH = 2
SPAN = 5
HEADS = 8
MESH = pl.DeviceIdType.MESH


def places():
    n, h, size = lax.axis_index("node"), lax.axis_index("head"), lax.axis_size("node")
    return n, h, lax.rem(n + 1, size), lax.rem(n + size - 1, size)


def greet(n, h, up, down):
    barrier = pltpu.get_barrier_semaphore()
    for r in range(1, HEADS):
        pl.semaphore_signal(barrier, inc=1, device_id=(n, lax.rem(h + r, HEADS)), device_id_type=MESH)
    for other in (up, down):
        pl.semaphore_signal(barrier, inc=1, device_id=(other, h), device_id_type=MESH)
    pl.semaphore_wait(barrier, HEADS + 1)


def send(src, dst, ssem, rsem, device):
    return pltpu.make_async_remote_copy(src_ref=src, dst_ref=dst, send_sem=ssem, recv_sem=rsem, device_id=device, device_id_type=MESH)


def columns(c):
    return pl.ds(pl.multiple_of(c * CL, CL), CL)


def fetch_kernel(k, v, q, g, nk, nv, oq, og, lsem, asend, arecv, fsend, frecv):
    n, h, up, down = places()
    sources = (k, v, q, g)
    own = (nk.at[REACH], nv.at[REACH], oq, og)
    near = (nk, nv)

    def local(a):
        return pltpu.make_async_copy(sources[a].at[:, columns(h)], own[a].at[h], lsem.at[a])

    def across(a, r):
        to = lax.rem(h + r, HEADS)
        return send(sources[a].at[:, columns(to)], own[a].at[h], asend.at[a, r], arecv.at[a, r], (n, to))

    def step(a, way, r):
        c = lax.rem(h + HEADS - r, HEADS)
        start, end = ((2, 1), (2, 3), (1, 0), (3, 4))[way]
        return send(near[a].at[start, c], near[a].at[end, c], fsend.at[a, way, r], frecv.at[a, way, r], (down if way % 2 else up, h))

    for a in range(4):
        local(a).start()
    greet(n, h, up, down)

    def loop(first, body):
        def run(r, carry):
            body(r)
            return carry
        lax.fori_loop(first, HEADS, run, 0)

    for a in range(4):
        loop(1, lambda r: across(a, r).start())
    for a in range(2):
        local(a).wait()
        step(a, 0, 0).start()
        step(a, 1, 0).start()

        def on(r):
            across(a, r).wait_recv()
            step(a, 0, r).start()
            step(a, 1, r).start()
        loop(1, on)
    for a in range(2):
        def relay(r):
            step(a, 0, r).wait_recv()
            step(a, 2, r).start()
            step(a, 1, r).wait_recv()
            step(a, 3, r).start()
        loop(0, relay)
    for a in range(2, 4):
        local(a).wait()
        loop(1, lambda r: across(a, r).wait_recv())
    for a in range(4):
        loop(1, lambda r: across(a, r).wait_send())
    for a in range(2):
        def last(r):
            step(a, 2, r).wait_recv()
            step(a, 3, r).wait_recv()
            for way in range(4):
                step(a, way, r).wait_send()
        loop(0, last)


def fetch(k, v, q, g):
    bf = jnp.bfloat16
    anywhere = pl.BlockSpec(memory_space=pl.ANY)
    near = jax.ShapeDtypeStruct((SPAN, HEADS, CL, CL), bf)
    own = jax.ShapeDtypeStruct((HEADS, CL, CL), bf)
    dma = pltpu.SemaphoreType.DMA
    return pl.pallas_call(
        fetch_kernel,
        out_shape=(near, near, own, own),
        in_specs=[anywhere] * 4,
        out_specs=(anywhere,) * 4,
        scratch_shapes=[dma((4,)), dma((4, HEADS)), dma((4, HEADS)), dma((2, 4, HEADS)), dma((2, 4, HEADS))],
        compiler_params=pltpu.CompilerParams(collective_id=0, has_side_effects=True),
    )(k, v, q, g)


def give_kernel(gk, gv, gq, ok, ov, oq, came, left, total, lsem, asend, arecv, fsend, frecv):
    n, h, up, down = places()
    parts = (gk, gv)
    outs = (ok, ov, oq)

    def final(a, c):
        return gq.at[c] if a == 2 else total.at[a, c]

    def local(a):
        return pltpu.make_async_copy(final(a, h), outs[a].at[:, columns(h)], lsem.at[a])

    def across(a, r):
        to = lax.rem(h + r, HEADS)
        return send(final(a, to), outs[a].at[:, columns(h)], asend.at[a, r], arecv.at[a, r], (n, to))

    def step(a, way, r):
        c = lax.rem(h + r, HEADS)
        src = (parts[a].at[4, c], parts[a].at[0, c], left.at[a, 0, c], left.at[a, 1, c])[way]
        return send(src, came.at[a, way, c], fsend.at[a, way, r], frecv.at[a, way, r], (down if way % 2 else up, h))

    def loop(first, body):
        def run(r, carry):
            body(r)
            return carry
        lax.fori_loop(first, HEADS, run, 0)

    def add(*terms):
        acc = terms[0].astype(jnp.float32)
        for t in terms[1:]:
            acc = acc + t.astype(jnp.float32)
        return acc.astype(jnp.bfloat16)

    greet(n, h, up, down)
    local(2).start()
    for a in range(2):
        def out(r):
            step(a, 0, r).start()
            step(a, 1, r).start()
        loop(0, out)
    loop(1, lambda r: across(2, r).start())
    for a in range(2):
        def relay(r):
            c = lax.rem(h + r, HEADS)
            step(a, 0, r).wait_recv()
            left[a, 0, c] = add(parts[a][3, c], came[a, 0, c])
            step(a, 2, r).start()
            step(a, 1, r).wait_recv()
            left[a, 1, c] = add(parts[a][1, c], came[a, 1, c])
            step(a, 3, r).start()
        loop(0, relay)
    for a in range(2):
        def finish(r):
            c = lax.rem(h + r, HEADS)
            step(a, 2, r).wait_recv()
            step(a, 3, r).wait_recv()
            total[a, c] = add(parts[a][2, c], came[a, 2, c], came[a, 3, c])
        finish(0)
        local(a).start()

        def rest(r):
            finish(r)
            across(a, r).start()
        loop(1, rest)
    for a in range(3):
        local(a).wait()

        def end(r):
            across(a, r).wait_recv()
            across(a, r).wait_send()
        loop(1, end)
    for a in range(2):
        def sent(r):
            for way in range(4):
                step(a, way, r).wait_send()
        loop(0, sent)


def give(gk, gv, gq):
    bf = jnp.bfloat16
    anywhere = pl.BlockSpec(memory_space=pl.ANY)
    inside = pl.BlockSpec(memory_space=pltpu.VMEM)
    out = jax.ShapeDtypeStruct((CL, HEADS * CL), bf)
    dma = pltpu.SemaphoreType.DMA
    return pl.pallas_call(
        give_kernel,
        out_shape=(out, out, out),
        in_specs=[inside] * 3,
        out_specs=(anywhere,) * 3,
        scratch_shapes=[pltpu.VMEM((2, 4, HEADS, CL, CL), bf), pltpu.VMEM((2, 2, HEADS, CL, CL), bf), pltpu.VMEM((2, HEADS, CL, CL), bf), dma((3,)), dma((3, HEADS)), dma((3, HEADS)), dma((2, 4, HEADS)), dma((2, 4, HEADS))],
        compiler_params=pltpu.CompilerParams(collective_id=1, has_side_effects=True),
    )(gk, gv, gq)


def on_device(query_rows, key_rows, value_rows, grad_out, heat_bias, block_pattern):
    near_k, near_v, q, g = fetch(key_rows, value_rows, query_rows, grad_out)
    shard = lax.axis_index("node")
    index = jnp.where(block_pattern < 0, -1, block_pattern - (shard - REACH) * CPN).reshape(-1)
    shape = (SPAN * HEADS, CL, CL)
    gq, gk, gv = attend(index, q, g, heat_bias, near_k.reshape(shape), near_v.reshape(shape))
    shape = (SPAN, HEADS, CL, CL)
    grad_key, grad_value, grad_query = give(gk.reshape(shape), gv.reshape(shape), gq)
    return grad_query, grad_key, grad_value


def solution(mesh):
    rows = P(("node", "head"), None)
    return jax.shard_map(
        on_device,
        mesh=mesh,
        in_specs=(rows, rows, rows, rows, P("node", None, None, None), P("node", None)),
        out_specs=(rows, rows, rows),
        check_vma=False,
    )
```
